512 devices in a mesh: batch: 16 (over y, core), seq: 32 (over x, z).
Axes of the slice: x: 4, y: 8, z: 8, core: 2. Of those that a mesh axis runs over, the one named last changes fastest.
Arguments:
- tokens: bfloat16 [16, 16384, 768], P('batch', 'seq'), may hold values from -6 to 6
- slide_lengths: int32 [16], P('batch'), may hold values from 2048 to 16384, as said below
- conv_weight: float32 [5, 768], replicated, may hold values from -2.5 to 2.5
- norm_gain: float32 [768], replicated, may hold values from 0.1 to 1.9
- w_query: bfloat16 [768, 768], P('batch'), may hold values from -8 to 8
- w_keyvalue: bfloat16 [768, 1536], P('batch'), may hold values from -0.21875 to 0.21875
- w_out: bfloat16 [768, 768], P('batch'), may hold values from -0.625 to 0.625
Outputs:
- result: bfloat16 [16, 16384, 768], P('batch', 'seq')
The draws below stay inside these ranges and needn't reach their ends.
Inputs may be any that keep to these rules, and one draw needn't show every extreme that they name: `slide_lengths`: some slide uses all 16384 token slots.
All inputs are finite; a program needn't handle non-finite values.
Results may differ from the reference program's by a relative error of at most 0.0055.
The reference program's roundings to bfloat16 on the way count: a program that leaves them out, or rounds other values in their place, can miss the bound.
Values may be sent and summed in bfloat16 or wider, within the bound.
A program may use at most 64 MiB of HBM per device.

```python
import math
import jax
import jax.numpy as jnp
from jax import lax

D = 768
HEADS = 12
HEAD_DIM = 64
TOK_DEV = 512
GROUP = 4
CONV_TAP_COUNT = 5
CONV_DILATION = 3
SEG0 = 512
SLIDE = 16384
SLIDES = 16
N_SEQ = 32


def draw_slide_lengths(key, part):
    lengths = jax.random.randint(key, (SLIDES,), SLIDE // 8, SLIDE + 1, dtype=jnp.int32)
    chosen = jax.random.randint(jax.random.fold_in(key, 11), (), 0, SLIDES, dtype=jnp.int32)
    return jnp.where(jnp.arange(SLIDES, dtype=jnp.int32) == chosen, SLIDE, lengths).astype(jnp.int32)


def draw_w_query(key, part):
    base = jax.random.truncated_normal(key, -4.0, 4.0, (D, D), jnp.float32) * (1.0 / math.sqrt(D))
    unit = jax.random.uniform(jax.random.fold_in(key, 5), (HEADS,), jnp.float32)
    scale = jnp.exp(unit * math.log(4.0))
    column_scale = jnp.repeat(scale, D // HEADS)
    return (base * column_scale[None, :]).astype(jnp.bfloat16)


def levels(rng, extent, pieces, smallest, top_value):
    level = 1.0
    for dim, shards_of in pieces:
        steps = jax.random.uniform(jax.random.fold_in(jax.random.fold_in(rng, 6), dim), (shards_of,), jnp.float32, smallest / len(pieces), top_value / len(pieces))
        level = level * jnp.repeat(jnp.exp(steps), extent[dim] // shards_of).reshape((-1,) + (1,) * (len(extent) - 1 - dim))
    return level


def scatter_about(stream_key, extent, spread, bound, shards=(), kind=jnp.bfloat16):
    entries = spread * jax.random.normal(stream_key, extent, jnp.float32)
    if shards:
        entries = entries * levels(stream_key, extent, shards, -0.22, 0.18)
    return jnp.clip(entries, -bound, bound).astype(kind)


def setup_inputs(seed: int = 0) -> dict:
    seeds = jax.random.split(jax.random.key(seed), 8)
    return {
        "tokens": scatter_about(seeds[0], (SLIDES, SLIDE, D), 1.0, 6.0, ((0, 16), (1, 32))),
        "slide_lengths": draw_slide_lengths(jax.random.fold_in(seeds[7], 71), 0),
        "conv_weight": scatter_about(seeds[2], (CONV_TAP_COUNT, D), 0.4, 2.5, (), jnp.float32),
        "norm_gain": jnp.clip(1.0 + 0.18 * jax.random.normal(seeds[3], (D,), jnp.float32), 0.1, 1.9),
        "w_query": draw_w_query(jax.random.fold_in(seeds[7], 71), 0),
        "w_keyvalue": scatter_about(seeds[5], (D, 2 * D), D ** -0.5, 0.21875, ((0, 16),)),
        "w_out": scatter_about(seeds[6], (D, D), (D // 8) ** -0.5, 0.625, ((0, 16),)),
    }


def attend(query_vectors, key_vectors, value_vectors, usable):
    score_matrix = jnp.einsum('ftl,fhl->fth', query_vectors.astype(jnp.float32), key_vectors.astype(jnp.float32))
    score_matrix = jnp.where(usable[:, None, :], score_matrix, -1000000000.0)
    row_max = lax.optimization_barrier(jnp.max(score_matrix, axis=-1))
    exponent = jnp.exp(score_matrix - row_max[..., None])
    row_sum = lax.optimization_barrier(jnp.sum(exponent, axis=-1))
    attention_weights = lax.optimization_barrier(exponent.astype(jnp.bfloat16))
    weighted_values = jnp.einsum('hcp,hpu->hcu', attention_weights.astype(jnp.float32), value_vectors.astype(jnp.float32))
    return (weighted_values / row_sum[..., None], row_max + jnp.log(row_sum))

def reference(tokens, slide_lengths, conv_weight, norm_gain, w_query, w_keyvalue, w_out):

    def one_slide(item_tuple):
        slide_tokens, slide_length = item_tuple
        position = jnp.arange(SLIDE, dtype=jnp.int32)
        live_rows = position < slide_length
        masked = jnp.where(live_rows[:, None], slide_tokens, jnp.zeros_like(slide_tokens))
        border_padding = CONV_DILATION * (CONV_TAP_COUNT // 2)
        padded = jnp.pad(masked.astype(jnp.float32), ((border_padding, border_padding), (0, 0)))
        mixed_rows = masked.astype(jnp.float32)
        for filter_tap_index in range(CONV_TAP_COUNT):
            tap_shift_amount = border_padding + (filter_tap_index - CONV_TAP_COUNT // 2) * CONV_DILATION
            mixed_rows = mixed_rows + conv_weight[filter_tap_index] * padded[tap_shift_amount:tap_shift_amount + SLIDE]
        average = lax.optimization_barrier(jnp.mean(mixed_rows, axis=-1, keepdims=True))
        centered = mixed_rows - average
        variance = lax.optimization_barrier(jnp.mean(centered * centered, axis=-1, keepdims=True))
        normed = (centered * lax.rsqrt(variance + 1e-05) * norm_gain).astype(jnp.bfloat16)
        query_vectors = (jnp.dot(normed, w_query, preferred_element_type=jnp.float32) * (1.0 / math.sqrt(HEAD_DIM))).astype(jnp.bfloat16)
        key_value = jnp.dot(normed, w_keyvalue, preferred_element_type=jnp.float32).astype(jnp.bfloat16)
        key_vectors = key_value[:, :D]
        value_vectors = key_value[:, D:]
        plan = ((SEG0, 1), (GROUP * TOK_DEV, GROUP), (SLIDE, N_SEQ))
        head_outputs = []
        for head in range(HEADS):
            low = head * HEAD_DIM
            high = low + HEAD_DIM
            results = []
            for segment, rate in plan:
                tap_shift_amount = head % rate
                count = segment // rate
                blocks = SLIDE // segment
                query_rows = query_vectors[tap_shift_amount::rate, low:high].reshape(blocks, count, HEAD_DIM)
                key_rows = key_vectors[tap_shift_amount::rate, low:high].reshape(blocks, count, HEAD_DIM)
                value_rows = value_vectors[tap_shift_amount::rate, low:high].reshape(blocks, count, HEAD_DIM)
                usable = live_rows[tap_shift_amount::rate].reshape(blocks, count)
                outputs, log_total = attend(query_rows, key_rows, value_rows, usable)
                full_out = jnp.zeros((SLIDE, HEAD_DIM), jnp.float32).at[tap_shift_amount::rate].set(outputs.reshape(-1, HEAD_DIM))
                full_log = jnp.full((SLIDE,), -jnp.inf, jnp.float32).at[tap_shift_amount::rate].set(log_total.reshape(-1))
                results.append((full_out, full_log))
            highest = jnp.maximum(jnp.maximum(results[0][1], results[1][1]), results[2][1])
            factors = [jnp.exp(entry[1] - highest) for entry in results]
            numer = factors[0][:, None] * results[0][0] + factors[1][:, None] * results[1][0] + factors[2][:, None] * results[2][0]
            denom = factors[0] + factors[1] + factors[2]
            head_outputs.append(jnp.where(live_rows[:, None], numer / denom[:, None], 0.0))
        attention = jnp.concatenate(head_outputs, axis=1).astype(jnp.bfloat16)
        return jnp.dot(attention, w_out, preferred_element_type=jnp.float32).astype(jnp.bfloat16)
    return lax.map(one_slide, (tokens, slide_lengths))
```

```python
import jax
import jax.numpy as jnp
from jax import lax
from jax.experimental import pallas as pl
from jax.experimental.pallas import tpu as pltpu
from jax.sharding import PartitionSpec as P

HEADS = 12
HEAD = 64
D = 768
ROWS = 512
TAPS = 5
DIL = 3
NY = 8
NX = 4
NZ = 8
SH = 48
CW = 640
PAD = 16
NEG = -1e9
F32 = jnp.float32
BF = jnp.bfloat16
MESH = pl.DeviceIdType.MESH


def lanes(shape):
    return lax.broadcasted_iota(jnp.int32, shape, len(shape) - 1)


def dot_nt(a, b):
    return lax.dot_general(a, b, (((1,), (1,)), ((), ())), preferred_element_type=F32)


def softmax_block(q, kv, bias):
    s = dot_nt(q, kv) + bias
    m = jnp.max(s, axis=1, keepdims=True)
    e = jnp.exp(s - m)
    total = jnp.sum(e, axis=1, keepdims=True)
    o = jnp.dot(e.astype(BF), kv, preferred_element_type=F32)
    return o / total, m + jnp.log(total)


def attend3(qa, qb, kv, bias):
    low = lanes(qa.shape) < HEAD
    zero = jnp.zeros_like(qa)
    o0, l0 = softmax_block(jnp.where(low, qa, zero), kv(0), bias)
    o1, l1 = softmax_block(jnp.where(low, zero, qa), kv(1), bias)
    o2, l2 = softmax_block(qb, kv(2), bias)
    flow = lanes(o0.shape) < HEAD
    return (
        jnp.where(flow, o1, o0),
        jnp.where(flow, 0.0, o2),
        jnp.where(flow, l1, l0),
        jnp.broadcast_to(l2, o2.shape),
    )


def split_log(value, lane):
    hi = value.astype(BF).astype(F32)
    rest = value - hi
    mid = rest.astype(BF).astype(F32)
    lo = rest - mid
    place = lane % 16
    return jnp.where(
        place == 0, hi, jnp.where(place == 1, mid, jnp.where(place == 2, lo, 0.0))
    )


def kernel(
    tok_ref,
    len_ref,
    cw_ref,
    gain_ref,
    wq_ref,
    wkv_ref,
    wo_ref,
    out_ref,
    wfull,
    woutf,
    woutp,
    xp,
    hl,
    hr,
    xn,
    kvq,
    mid,
    slp,
    sl,
    oret,
    ret,
    sret,
    srt,
    attn,
    dout,
    dlog,
    outf,
    ring_s,
    ring_r,
    sib_s,
    sib_r,
    halo_s,
    halo_r,
    a2a_s,
    a2a_r,
    slz_s,
    slz_r,
    slo_s,
    slo_r,
    slx_s,
    slx_r,
    ret_s,
    ret_r,
    srt_s,
    srt_r,
):
    b = lax.axis_index("batch")
    q = lax.axis_index("seq")
    y = b // 2
    c = b % 2
    x = q // NZ
    z = q % NZ
    zr = z % 4
    zg = z // 4
    length = len_ref[0]
    first = q * ROWS

    barrier = pltpu.get_barrier_semaphore()
    friends = [
        (2 * ((y + 1) % NY) + c, q),
        (2 * ((y + NY - 1) % NY) + c, q),
        (2 * y + 1 - c, q),
        (b, (q + 1) % 32),
        (b, (q + 31) % 32),
    ]
    friends += [(b, x * NZ + (z + i) % NZ) for i in range(1, NZ)]
    friends += [(b, ((x + i) % NX) * NZ + z) for i in range(1, NX)]
    for friend in friends:
        pl.semaphore_signal(barrier, inc=1, device_id=friend, device_id_type=MESH)

    own_rows = pl.ds(pl.multiple_of(b * SH, 16), SH)
    wlane = lanes((SH, 128)) < HEAD

    def half(ref, col, upper):
        block = ref[:, (col // 128) * 128 : (col // 128) * 128 + 128].astype(F32)
        if (col % 128 == HEAD) != upper:
            block = pltpu.roll(block, HEAD, 1)
        return block

    def place(r, i, low, high):
        wfull[r, own_rows, 128 * i : 128 * i + 128] = jnp.where(wlane, low, high).astype(BF)

    for r in range(4):
        h0, h1, h2 = HEAD * r, HEAD * (r + 4), HEAD * (r + 8)
        place(r, 0, half(wkv_ref, h0, False), half(wkv_ref, D + h0, True))
        place(r, 1, half(wkv_ref, D + h1, False), half(wkv_ref, h1, True))
        place(r, 2, half(wkv_ref, h2, False), half(wkv_ref, D + h2, True))
        place(r, 3, half(wq_ref, h0, False), half(wq_ref, h1, True))
        place(r, 4, half(wq_ref, h2, False), jnp.zeros((SH, 128), F32))
    woutf[own_rows, :] = wo_ref[...]

    def cls(g):
        return (zr + g + 1) % 4

    way = 1 - 2 * c

    def shard(ch, yo, co):
        rows = pl.ds(pl.multiple_of((2 * yo + co) * SH, 16), SH)
        if ch < 4:
            return wfull.at[cls(ch), rows, :]
        return woutf.at[rows, :]

    def ring_copy(ch, long, k):
        d = way if long else -way
        part = shard(ch, (y + NY - k * d) % NY, c)
        i = k if long else 4 + k
        return pltpu.make_async_remote_copy(
            src_ref=part,
            dst_ref=part,
            send_sem=ring_s.at[ch, i],
            recv_sem=ring_r.at[ch, i],
            device_id=(2 * ((y + NY + d) % NY) + c, q),
            device_id_type=MESH,
        )

    def sib_copy(ch, i):
        step = -i * way if i <= 4 else (i - 4) * way
        part = shard(ch, (y + NY + step) % NY, c)
        return pltpu.make_async_remote_copy(
            src_ref=part,
            dst_ref=part,
            send_sem=sib_s.at[ch, i],
            recv_sem=sib_r.at[ch, i],
            device_id=(2 * y + 1 - c, q),
            device_id_type=MESH,
        )

    def event(ch, k):
        if ch > 4:
            return
        if k == 0:
            ring_copy(ch, True, 0).start()
            ring_copy(ch, False, 0).start()
            sib_copy(ch, 0).start()
            return
        ring_copy(ch, True, k - 1).wait_recv()
        if k <= 3:
            ring_copy(ch, True, k).start()
        sib_copy(ch, k).start()
        if k <= 3:
            ring_copy(ch, False, k - 1).wait_recv()
            if k <= 2:
                ring_copy(ch, False, k).start()
            sib_copy(ch, 4 + k).start()

    def complete(ch):
        for i in range(8):
            sib_copy(ch, i).wait_recv()

    def halo_copy(right):
        if right:
            src, dst, i, to = tok_ref.at[0, pl.ds(ROWS - PAD, PAD), :], hl, 0, (q + 1) % 32
        else:
            src, dst, i, to = tok_ref.at[0, pl.ds(0, PAD), :], hr, 1, (q + 31) % 32
        return pltpu.make_async_remote_copy(
            src_ref=src,
            dst_ref=dst,
            send_sem=halo_s.at[i],
            recv_sem=halo_r.at[i],
            device_id=(b, to),
            device_id_type=MESH,
        )

    pl.semaphore_wait(barrier, len(friends))
    event(0, 0)
    halo_copy(True).start()
    halo_copy(False).start()
    event(1, 0)

    for i in range(6):
        cols = slice(128 * i, 128 * i + 128)
        pos = first + lax.broadcasted_iota(jnp.int32, (ROWS, 128), 0)
        xp[i, PAD : PAD + ROWS, :] = jnp.where(
            pos < length, tok_ref[0, :, cols].astype(F32), 0.0
        )

    def conv(s):
        parts = []
        for i in range(6):
            cols = slice(128 * i, 128 * i + 128)
            acc = xp[i, pl.ds(PAD + s, 16, stride=32), :]
            for t in range(TAPS):
                tap = xp[i, pl.ds(PAD + s + (t - TAPS // 2) * DIL, 16, stride=32), :]
                acc = acc + cw_ref[t : t + 1, cols] * tap
            parts.append(acc)
        total = parts[0]
        for part in parts[1:]:
            total = total + part
        mean = jnp.sum(total, axis=1, keepdims=True) * (1.0 / D)
        parts = [part - mean for part in parts]
        square = parts[0] * parts[0]
        for part in parts[1:]:
            square = square + part * part
        scale = lax.rsqrt(jnp.sum(square, axis=1, keepdims=True) * (1.0 / D) + 1e-5)
        row = pl.multiple_of(((s % 4) * 8 + s // 4) * 16, 16)
        for i in range(6):
            cols = slice(128 * i, 128 * i + 128)
            xn[pl.ds(row, 16), cols] = (parts[i] * scale * gain_ref[:, cols]).astype(BF)

    def conv_range(lo, hi):
        def step(s, carry):
            conv(s)
            return carry

        lax.fori_loop(lo, hi, step, 0)

    conv_range(6, 16)
    event(0, 1)
    conv_range(16, 26)
    event(0, 2)
    event(1, 1)
    halo_copy(True).wait_recv()
    halo_copy(False).wait_recv()
    for i in range(6):
        cols = slice(128 * i, 128 * i + 128)
        off = lax.broadcasted_iota(jnp.int32, (PAD, 128), 0)
        left = first - PAD + off
        right = first + ROWS + off
        left_ok = jnp.where(left >= 0, left, length) < length
        xp[i, 0:PAD, :] = jnp.where(left_ok, hl[:, cols].astype(F32), 0.0)
        xp[i, PAD + ROWS : 2 * PAD + ROWS, :] = jnp.where(
            right < length, hr[:, cols].astype(F32), 0.0
        )
    conv_range(0, 6)
    event(0, 3)
    event(1, 2)
    event(2, 0)
    conv_range(26, 32)
    event(0, 4)
    complete(0)

    def project(g):
        cg = cls(g)

        def step(i, carry):
            rows = pl.ds(pl.multiple_of(i * 256, 256), 256)
            res = jnp.dot(xn[rows, :], wfull[cg], preferred_element_type=F32)
            res = jnp.where(lanes(res.shape) < 384, res, res * (1.0 / 8.0))
            kvq[g, rows, :] = res.astype(BF)
            return carry

        lax.fori_loop(0, 2, step, 0)

    def cls_rows(g):
        return pl.ds(pl.multiple_of(cls(g) * 128, 128), 128)

    def a2a_copy(g):
        return pltpu.make_async_remote_copy(
            src_ref=kvq.at[g, cls_rows(g), :],
            dst_ref=mid.at[zr],
            send_sem=a2a_s.at[g],
            recv_sem=a2a_r.at[g],
            device_id=(b, x * NZ + zg * 4 + cls(g)),
            device_id_type=MESH,
        )

    def slz_copy(g):
        return pltpu.make_async_remote_copy(
            src_ref=slp.at[g],
            dst_ref=sl.at[x, z],
            send_sem=slz_s.at[g],
            recv_sem=slz_r.at[g],
            device_id=(b, x * NZ + zg * 4 + cls(g)),
            device_id_type=MESH,
        )

    def slo_copy(g):
        return pltpu.make_async_remote_copy(
            src_ref=slp.at[g],
            dst_ref=sl.at[x, z],
            send_sem=slo_s.at[g],
            recv_sem=slo_r.at[g],
            device_id=(b, x * NZ + (1 - zg) * 4 + cls(g)),
            device_id_type=MESH,
        )

    def slx_copy(i):
        return pltpu.make_async_remote_copy(
            src_ref=sl.at[x],
            dst_ref=sl.at[x],
            send_sem=slx_s.at[i],
            recv_sem=slx_r.at[i],
            device_id=(b, ((x + i + 1) % NX) * NZ + z),
            device_id_type=MESH,
        )

    def back(g):
        return (b, x * NZ + zg * 4 + (zr + 3 - g) % 4)

    def ret_copy(g):
        return pltpu.make_async_remote_copy(
            src_ref=oret.at[g],
            dst_ref=ret.at[g],
            send_sem=ret_s.at[g],
            recv_sem=ret_r.at[g],
            device_id=back(g),
            device_id_type=MESH,
        )

    def srt_copy(g):
        return pltpu.make_async_remote_copy(
            src_ref=sret.at[g],
            dst_ref=srt.at[g],
            send_sem=srt_s.at[g],
            recv_sem=srt_r.at[g],
            device_id=back(g),
            device_id_type=MESH,
        )

    def send_class(g):
        cg = cls(g)
        for u in range(3):
            rows = pl.ds(pl.multiple_of(cg * 128 + 16 * u, 16), 16)
            tile = kvq[g, rows, 128 * u : 128 * u + 128]
            slp[g, u] = tile
            if g == 3:
                sl[x, z, u] = tile
        slo_copy(g).start()
        if g < 3:
            slz_copy(g).start()
            a2a_copy(g).start()
        else:
            mid[zr] = kvq[g, cls_rows(g), :]

    key = lax.broadcasted_iota(jnp.int32, (1, ROWS), 1)
    inner = 32 * (key % 16) + 4 * ((key // 16) % 8)
    dense_bias = jnp.where(first + inner + key // 128 < length, 0.0, NEG)

    def live(r, width):
        row = lax.broadcasted_iota(jnp.int32, (128, width), 0)
        return first + 32 * (row % 16) + 4 * (row // 16) + r < length

    def dense(g, lo, hi):
        cg = cls(g)

        def step(i, carry):
            r = (cg + i) % 4
            rows = pl.ds(pl.multiple_of(r * 128, 128), 128)
            o0, o1, l0, l1 = attend3(
                kvq[g, rows, 384:512],
                kvq[g, rows, 512:640],
                lambda u: kvq[g, :, 128 * u : 128 * u + 128],
                dense_bias,
            )
            ok = live(r, 128)
            attn[cg, rows, 0:128] = jnp.where(ok, o0, 0.0).astype(BF)
            attn[cg, rows, 128:256] = jnp.where(ok, o1, 0.0).astype(BF)

            @pl.when(i == 0)
            def _():
                dout[g, :, 0:128] = o0
                dout[g, :, 128:256] = o1
                dlog[g, :, 0:128] = l0
                dlog[g, :, 128:256] = l1

            return carry

        lax.fori_loop(lo, hi, step, 0)

    for g in range(4):
        project(g)
        send_class(g)
        event(g + 1, 3)
        event(g + 2, 1)
        dense(g, 0, 2)
        event(g + 1, 4)
        event(g + 2, 2)
        event(g + 3, 0)
        dense(g, 2, 4)
        if g < 3:
            complete(g + 1)

    for g in range(3):
        slz_copy(g).wait_recv()
    for g in range(4):
        slo_copy(g).wait_recv()
    for i in range(3):
        slx_copy(i).start()

    for g in range(3):
        a2a_copy(g).wait_recv()
    group_first = (q // 4) * 4 * ROWS
    mid_bias = jnp.where(group_first + 512 * (key // 128) + inner + zr < length, 0.0, NEG)

    def mid_step(g, carry):
        m = (zr + 3 - g) % 4
        o0, o1, l0, l1 = attend3(
            mid[m, :, 384:512],
            mid[m, :, 512:640],
            lambda u: mid[:, :, 128 * u : 128 * u + 128].reshape(ROWS, 128),
            mid_bias,
        )
        lane = lanes(o0.shape)
        logs = jnp.where(
            lane < 16, pltpu.roll(l0, HEAD, 1), jnp.where(lane < 32, l0, l1)
        )
        logs = jnp.where(lane < 48, split_log(logs, lane), 0.0)
        oret[g, :, 0:128] = o0.astype(BF)
        oret[g, :, 128:256] = jnp.where(lane < HEAD, logs, o1).astype(BF)

        @pl.when(g < 3)
        def _():
            ret_copy(g).start()

        return carry

    lax.fori_loop(0, 4, mid_step, 0)

    for i in range(3):
        slx_copy(i).wait_recv()
    lane64 = lanes((64, 128))
    for u in range(3):
        low = 0 if u != 1 else HEAD
        blk = slice(384, 512) if u < 2 else slice(512, 640)
        qs = mid[:, 16 * u : 16 * u + 16, blk].reshape(64, 128)
        mine = jnp.where(low == 0, lane64, lane64 - HEAD + 128) % 128 < HEAD
        qs = jnp.where(mine, qs, jnp.zeros_like(qs))
        kv = sl[:, :, u].reshape(ROWS, 128)
        bias = jnp.where(32 * key + 4 * u + zr < length, 0.0, NEG)
        o, lg = softmax_block(qs, kv, bias)
        logs = split_log(jnp.broadcast_to(lg, o.shape), lane64)
        packed = jnp.where(mine, logs, o).astype(BF)
        for m in range(4):
            sret[(zr + 3 - m) % 4, u] = packed[16 * m : 16 * m + 16, :]
    for g in range(3):
        srt_copy(g).start()

    complete(4)
    for r in range(4):
        woutp[r, 0:64, :] = woutf[HEAD * (r + 4) : HEAD * (r + 5), :]
        woutp[r, 64:128, :] = woutf[HEAD * r : HEAD * (r + 1), :]
        woutp[r, 128:192, :] = jnp.zeros((64, D), BF)
        woutp[r, 192:256, :] = woutf[HEAD * (r + 8) : HEAD * (r + 9), :]

    def join(logs, outs):
        top = jnp.maximum(jnp.maximum(logs[0], logs[1]), logs[2])
        cs = [jnp.exp(lg - top) for lg in logs]
        num = cs[0] * outs[0] + cs[1] * outs[1] + cs[2] * outs[2]
        return num / (cs[0] + cs[1] + cs[2])

    lane128 = lanes((128, 128))
    lane16 = lanes((16, 128))
    flow = lane128 < HEAD

    def finish(g, mret, sr):
        cg = cls(g)
        rows = cls_rows(g)
        m0 = mret[:, 0:128].astype(F32)
        m1 = mret[:, 128:256].astype(F32)

        def mlog(u):
            hit = jnp.where((lane128 >= 16 * u) & (lane128 < 16 * u + 16), m1, 0.0)
            return jnp.sum(hit, axis=1, keepdims=True)

        ml0 = jnp.where(flow, mlog(1), mlog(0))
        ml1 = jnp.broadcast_to(mlog(2), (128, 128))
        souts = []
        slogs = []
        for u in range(3):
            val = sr(u).astype(F32)
            mine = lane16 >= HEAD if u == 1 else lane16 < HEAD
            first16 = lane16 % HEAD < 16
            lg = jnp.sum(jnp.where(mine & first16, val, 0.0), axis=1, keepdims=True)
            souts.append(jnp.where(mine, 0.0, val))
            slogs.append(jnp.where(mine, -1e30, lg))
        rest = jnp.zeros((80, 128), F32)
        z16 = jnp.zeros((16, 128), F32)
        n16 = jnp.full((16, 128), -1e30, F32)
        nrest = jnp.full((80, 128), -1e30, F32)
        s0 = jnp.concatenate([souts[0], souts[1], z16, rest], axis=0)
        sl0 = jnp.concatenate([slogs[0], slogs[1], n16, nrest], axis=0)
        s1 = jnp.concatenate([z16, z16, souts[2], rest], axis=0)
        sl1 = jnp.concatenate([n16, n16, slogs[2], nrest], axis=0)
        ok = live(cg, 128)
        a0 = join((dlog[g, :, 0:128], ml0, sl0), (dout[g, :, 0:128], m0, s0))
        a1 = join((dlog[g, :, 128:256], ml1, sl1), (dout[g, :, 128:256], m1, s1))
        a1 = jnp.where(flow, 0.0, a1)
        attn[cg, rows, 0:128] = jnp.where(ok, a0, 0.0).astype(BF)
        attn[cg, rows, 128:256] = jnp.where(ok, a1, 0.0).astype(BF)
        res = jnp.dot(attn[0, rows, :], woutp[0], preferred_element_type=F32)
        for r in range(1, 4):
            res = res + jnp.dot(attn[r, rows, :], woutp[r], preferred_element_type=F32)
        for v in range(8):
            for i in range(6):
                outf[i, pl.ds(4 * v + cg, 16, stride=32), :] = res[
                    16 * v : 16 * v + 16, 128 * i : 128 * i + 128
                ]

    finish(3, oret[3], lambda u: sret[3, u])
    for g in range(3):
        ret_copy(g).wait_recv()
        srt_copy(g).wait_recv()
        finish(g, ret[g], lambda u, g=g: srt[g, u])
    for i in range(6):
        out_ref[0, :, 128 * i : 128 * i + 128] = outf[i].astype(BF)

    for ch in range(5):
        for k in range(4):
            ring_copy(ch, True, k).wait_send()
        for k in range(3):
            ring_copy(ch, False, k).wait_send()
        for i in range(8):
            sib_copy(ch, i).wait_send()
    halo_copy(True).wait_send()
    halo_copy(False).wait_send()
    for g in range(3):
        a2a_copy(g).wait_send()
        slz_copy(g).wait_send()
        slx_copy(g).wait_send()
        ret_copy(g).wait_send()
        srt_copy(g).wait_send()
    for g in range(4):
        slo_copy(g).wait_send()


def on_device(tokens, slide_lengths, conv_weight, norm_gain, w_query, w_keyvalue, w_out):
    vmem = pl.BlockSpec(memory_space=pltpu.VMEM)
    dma = pltpu.SemaphoreType.DMA
    return pl.pallas_call(
        kernel,
        out_shape=jax.ShapeDtypeStruct((1, ROWS, D), BF),
        in_specs=[vmem, pl.BlockSpec(memory_space=pltpu.SMEM)] + [vmem] * 5,
        out_specs=vmem,
        scratch_shapes=[
            pltpu.VMEM((4, D, CW), BF),
            pltpu.VMEM((D, D), BF),
            pltpu.VMEM((4, 256, D), BF),
            pltpu.VMEM((6, ROWS + 2 * PAD, 128), F32),
            pltpu.VMEM((PAD, D), BF),
            pltpu.VMEM((PAD, D), BF),
            pltpu.VMEM((ROWS, D), BF),
            pltpu.VMEM((4, ROWS, CW), BF),
            pltpu.VMEM((4, 128, CW), BF),
            pltpu.VMEM((4, 3, 16, 128), BF),
            pltpu.VMEM((NX, NZ, 3, 16, 128), BF),
            pltpu.VMEM((4, 128, 256), BF),
            pltpu.VMEM((3, 128, 256), BF),
            pltpu.VMEM((4, 3, 16, 128), BF),
            pltpu.VMEM((3, 3, 16, 128), BF),
            pltpu.VMEM((4, ROWS, 256), BF),
            pltpu.VMEM((4, 128, 256), F32),
            pltpu.VMEM((4, 128, 256), F32),
            pltpu.VMEM((6, ROWS, 128), F32),
            dma((5, 7)),
            dma((5, 7)),
            dma((5, 8)),
            dma((5, 8)),
            dma((2,)),
            dma((2,)),
            dma((3,)),
            dma((3,)),
            dma((3,)),
            dma((3,)),
            dma((4,)),
            dma((4,)),
            dma((3,)),
            dma((3,)),
            dma((3,)),
            dma((3,)),
            dma((3,)),
            dma((3,)),
        ],
        compiler_params=pltpu.CompilerParams(
            collective_id=0, has_side_effects=True, vmem_limit_bytes=60 * 1024 * 1024
        ),
        name="layer",
    )(
        tokens,
        slide_lengths,
        conv_weight,
        norm_gain.reshape(1, D),
        w_query,
        w_keyvalue,
        w_out,
    )


def solution(mesh):
    return jax.shard_map(
        on_device,
        mesh=mesh,
        in_specs=(
            P("batch", "seq", None),
            P("batch"),
            P(),
            P(),
            P("batch", None),
            P("batch", None),
            P("batch", None),
        ),
        out_specs=P("batch", "seq", None),
        check_vma=False,
    )
```

```python
import jax
import jax.numpy as jnp
from jax import lax
from jax.experimental import pallas as pl
from jax.experimental.pallas import tpu as pltpu
from jax.sharding import PartitionSpec as P

HEADS = 12
HEAD = 64
D = 768
ROWS = 512
TAPS = 5
DIL = 3
NY = 8
NX = 4
NZ = 8
SH = 48
CW = 640
PAD = 16
NEG = -1e9
F32 = jnp.float32
BF = jnp.bfloat16
MESH = pl.DeviceIdType.MESH


def lanes(shape):
    return lax.broadcasted_iota(jnp.int32, shape, len(shape) - 1)


def dot_nt(a, b):
    return lax.dot_general(a, b, (((1,), (1,)), ((), ())), preferred_element_type=F32)


def softmax_block(q, kv, bias):
    s = dot_nt(q, kv) + bias
    m = jnp.max(s, axis=1, keepdims=True)
    e = jnp.exp(s - m)
    total = jnp.sum(e, axis=1, keepdims=True)
    o = jnp.dot(e.astype(BF), kv, preferred_element_type=F32)
    return o / total, m + jnp.log(total)


def attend3(qa, qb, kv, bias):
    low = lanes(qa.shape) < HEAD
    zero = jnp.zeros_like(qa)
    o0, l0 = softmax_block(jnp.where(low, qa, zero), kv(0), bias)
    o1, l1 = softmax_block(jnp.where(low, zero, qa), kv(1), bias)
    o2, l2 = softmax_block(qb, kv(2), bias)
    flow = lanes(o0.shape) < HEAD
    return (
        jnp.where(flow, o1, o0),
        jnp.where(flow, 0.0, o2),
        jnp.where(flow, l1, l0),
        jnp.broadcast_to(l2, o2.shape),
    )


def split_log(value, lane):
    hi = value.astype(BF).astype(F32)
    rest = value - hi
    mid = rest.astype(BF).astype(F32)
    lo = rest - mid
    place = lane % 16
    return jnp.where(
        place == 0, hi, jnp.where(place == 1, mid, jnp.where(place == 2, lo, 0.0))
    )


def kernel(
    tok_hbm,
    len_ref,
    cw_hbm,
    gain_hbm,
    wq_hbm,
    wkv_hbm,
    wo_hbm,
    out_ref,
    tok_ref,
    cw_ref,
    gain_ref,
    wq_ref,
    wkv_ref,
    wo_ref,
    in_s,
    wfull,
    woutf,
    woutp,
    xp,
    hl,
    hr,
    xn,
    kvq,
    mid,
    slp,
    sl,
    oret,
    ret,
    sret,
    srt,
    attn,
    dout,
    dlog,
    outf,
    ring_s,
    ring_r,
    sib_s,
    sib_r,
    halo_s,
    halo_r,
    a2a_s,
    a2a_r,
    slz_s,
    slz_r,
    slo_s,
    slo_r,
    slx_s,
    slx_r,
    ret_s,
    ret_r,
    srt_s,
    srt_r,
):
    b = lax.axis_index("batch")
    q = lax.axis_index("seq")
    y = b // 2
    c = b % 2
    x = q // NZ
    z = q % NZ
    zr = z % 4
    zg = z // 4
    length = len_ref[0]
    first = q * ROWS

    barrier = pltpu.get_barrier_semaphore()
    friends = [
        (2 * ((y + 1) % NY) + c, q),
        (2 * ((y + NY - 1) % NY) + c, q),
        (2 * y + 1 - c, q),
        (b, (q + 1) % 32),
        (b, (q + 31) % 32),
    ]
    friends += [(b, x * NZ + (z + i) % NZ) for i in range(1, NZ)]
    friends += [(b, ((x + i) % NX) * NZ + z) for i in range(1, NX)]
    for friend in friends:
        pl.semaphore_signal(barrier, inc=1, device_id=friend, device_id_type=MESH)

    loads = [
        pltpu.make_async_copy(src, dst, in_s.at[i])
        for i, (src, dst) in enumerate(
            (
                (wkv_hbm, wkv_ref),
                (wq_hbm, wq_ref),
                (wo_hbm, wo_ref),
                (tok_hbm, tok_ref),
                (cw_hbm, cw_ref),
                (gain_hbm, gain_ref),
            )
        )
    ]
    for load in loads:
        load.start()
    for load in loads[:3]:
        load.wait()

    own_rows = pl.ds(pl.multiple_of(b * SH, 16), SH)
    wlane = lanes((SH, 128)) < HEAD

    def half(ref, col, upper):
        block = ref[:, (col // 128) * 128 : (col // 128) * 128 + 128].astype(F32)
        if (col % 128 == HEAD) != upper:
            block = pltpu.roll(block, HEAD, 1)
        return block

    def place(r, i, low, high):
        wfull[r, own_rows, 128 * i : 128 * i + 128] = jnp.where(wlane, low, high).astype(BF)

    for r in range(4):
        h0, h1, h2 = HEAD * r, HEAD * (r + 4), HEAD * (r + 8)
        place(r, 0, half(wkv_ref, h0, False), half(wkv_ref, D + h0, True))
        place(r, 1, half(wkv_ref, D + h1, False), half(wkv_ref, h1, True))
        place(r, 2, half(wkv_ref, h2, False), half(wkv_ref, D + h2, True))
        place(r, 3, half(wq_ref, h0, False), half(wq_ref, h1, True))
        place(r, 4, half(wq_ref, h2, False), jnp.zeros((SH, 128), F32))
    woutf[own_rows, :] = wo_ref[...]

    def cls(g):
        return (zr + g + 1) % 4

    def mask_tokens():
        for j in range(16):
            pos = first + 32 * j + lax.broadcasted_iota(jnp.int32, (32, 128), 0)
            ok = pos < length
            for i in range(6):
                tile = tok_ref[0, 32 * j : 32 * j + 32, 128 * i : 128 * i + 128]
                xp[i, 33 * j + 33 : 33 * j + 65, :] = jnp.where(ok, tile.astype(F32), 0.0)

    way = 1 - 2 * c

    def shard(ch, yo, co):
        rows = pl.ds(pl.multiple_of((2 * yo + co) * SH, 16), SH)
        if ch < 4:
            return wfull.at[cls(ch), rows, :]
        return woutf.at[rows, :]

    def ring_copy(ch, long, k):
        d = way if long else -way
        part = shard(ch, (y + NY - k * d) % NY, c)
        i = k if long else 4 + k
        return pltpu.make_async_remote_copy(
            src_ref=part,
            dst_ref=part,
            send_sem=ring_s.at[ch, i],
            recv_sem=ring_r.at[ch, i],
            device_id=(2 * ((y + NY + d) % NY) + c, q),
            device_id_type=MESH,
        )

    def sib_copy(ch, i):
        step = -i * way if i <= 4 else (i - 4) * way
        part = shard(ch, (y + NY + step) % NY, c)
        return pltpu.make_async_remote_copy(
            src_ref=part,
            dst_ref=part,
            send_sem=sib_s.at[ch, i],
            recv_sem=sib_r.at[ch, i],
            device_id=(2 * y + 1 - c, q),
            device_id_type=MESH,
        )

    def event(ch, k):
        if ch > 4:
            return
        if k == 0:
            ring_copy(ch, True, 0).start()
            ring_copy(ch, False, 0).start()
            sib_copy(ch, 0).start()
            return
        ring_copy(ch, True, k - 1).wait_recv()
        if k <= 3:
            ring_copy(ch, True, k).start()
        sib_copy(ch, k).start()
        if k <= 3:
            ring_copy(ch, False, k - 1).wait_recv()
            if k <= 2:
                ring_copy(ch, False, k).start()
            sib_copy(ch, 4 + k).start()

    def complete(ch):
        for i in range(8):
            sib_copy(ch, i).wait_recv()

    def halo_copy(right):
        if right:
            src, dst, i, to = tok_ref.at[0, pl.ds(ROWS - PAD, PAD), :], hl, 0, (q + 1) % 32
        else:
            src, dst, i, to = tok_ref.at[0, pl.ds(0, PAD), :], hr, 1, (q + 31) % 32
        return pltpu.make_async_remote_copy(
            src_ref=src,
            dst_ref=dst,
            send_sem=halo_s.at[i],
            recv_sem=halo_r.at[i],
            device_id=(b, to),
            device_id_type=MESH,
        )

    for load in loads[3:]:
        load.wait()
    mask_tokens()
    pl.semaphore_wait(barrier, len(friends))
    event(0, 0)
    halo_copy(True).start()
    halo_copy(False).start()
    event(1, 0)

    def conv(s):
        parts = []
        for i in range(6):
            cols = slice(128 * i, 128 * i + 128)
            acc = xp[i, pl.ds(33 + s, 16, stride=33), :]
            for t in range(TAPS):
                at = 32 + s + (t - TAPS // 2) * DIL
                tap = xp[i, pl.ds(33 * (at // 32) + at % 32, 16, stride=33), :]
                acc = acc + cw_ref[t : t + 1, cols] * tap
            parts.append(acc)
        total = parts[0]
        for part in parts[1:]:
            total = total + part
        mean = jnp.sum(total, axis=1, keepdims=True) * (1.0 / D)
        parts = [part - mean for part in parts]
        square = parts[0] * parts[0]
        for part in parts[1:]:
            square = square + part * part
        scale = lax.rsqrt(jnp.sum(square, axis=1, keepdims=True) * (1.0 / D) + 1e-5)
        row = pl.multiple_of(((s % 4) * 8 + s // 4) * 16, 16)
        for i in range(6):
            cols = slice(128 * i, 128 * i + 128)
            xn[pl.ds(row, 16), cols] = (parts[i] * scale * gain_ref[cols].reshape(1, 128)).astype(BF)

    def conv_range(lo, hi):
        def step(s, carry):
            conv(lo + 2 * s)
            conv(lo + 2 * s + 1)
            return carry

        lax.fori_loop(0, (hi - lo) // 2, step, 0)

    conv_range(6, 16)
    event(0, 1)
    conv_range(16, 26)
    event(1, 1)
    event(2, 0)
    event(0, 2)
    halo_copy(True).wait_recv()
    halo_copy(False).wait_recv()
    for i in range(6):
        cols = slice(128 * i, 128 * i + 128)
        off = lax.broadcasted_iota(jnp.int32, (PAD, 128), 0)
        left = first - PAD + off
        right = first + ROWS + off
        left_ok = jnp.where(left >= 0, left, length) < length
        xp[i, 16:32, :] = jnp.where(left_ok, hl[:, cols].astype(F32), 0.0)
        xp[i, 561:577, :] = jnp.where(
            right < length, hr[:, cols].astype(F32), 0.0
        )
    conv_range(0, 6)
    event(1, 2)
    event(2, 1)
    event(0, 3)
    event(3, 0)
    conv_range(26, 32)
    event(1, 3)
    event(2, 2)
    event(0, 4)
    event(3, 1)
    event(4, 0)
    complete(0)

    def project(g):
        cg = cls(g)

        def step(i, carry):
            rows = pl.ds(pl.multiple_of(i * 256, 256), 256)
            res = jnp.dot(xn[rows, :], wfull[cg], preferred_element_type=F32)
            res = jnp.where(lanes(res.shape) < 384, res, res * (1.0 / 8.0))
            kvq[g, rows, :] = res.astype(BF)
            return carry

        lax.fori_loop(0, 2, step, 0)

    def cls_rows(g):
        return pl.ds(pl.multiple_of(cls(g) * 128, 128), 128)

    def a2a_copy(g):
        return pltpu.make_async_remote_copy(
            src_ref=kvq.at[g, cls_rows(g), :],
            dst_ref=mid.at[zr],
            send_sem=a2a_s.at[g],
            recv_sem=a2a_r.at[g],
            device_id=(b, x * NZ + zg * 4 + cls(g)),
            device_id_type=MESH,
        )

    def slz_copy(g):
        return pltpu.make_async_remote_copy(
            src_ref=slp.at[g],
            dst_ref=sl.at[x, z],
            send_sem=slz_s.at[g],
            recv_sem=slz_r.at[g],
            device_id=(b, x * NZ + zg * 4 + cls(g)),
            device_id_type=MESH,
        )

    def slo_copy(g):
        return pltpu.make_async_remote_copy(
            src_ref=slp.at[g],
            dst_ref=sl.at[x, z],
            send_sem=slo_s.at[g],
            recv_sem=slo_r.at[g],
            device_id=(b, x * NZ + (1 - zg) * 4 + cls(g)),
            device_id_type=MESH,
        )

    def slx_copy(i):
        return pltpu.make_async_remote_copy(
            src_ref=sl.at[x],
            dst_ref=sl.at[x],
            send_sem=slx_s.at[i],
            recv_sem=slx_r.at[i],
            device_id=(b, ((x + i + 1) % NX) * NZ + z),
            device_id_type=MESH,
        )

    def back(g):
        return (b, x * NZ + zg * 4 + (zr + 3 - g) % 4)

    def ret_copy(g):
        return pltpu.make_async_remote_copy(
            src_ref=oret.at[g],
            dst_ref=ret.at[g],
            send_sem=ret_s.at[g],
            recv_sem=ret_r.at[g],
            device_id=back(g),
            device_id_type=MESH,
        )

    def srt_copy(g):
        return pltpu.make_async_remote_copy(
            src_ref=sret.at[g],
            dst_ref=srt.at[g],
            send_sem=srt_s.at[g],
            recv_sem=srt_r.at[g],
            device_id=back(g),
            device_id_type=MESH,
        )

    def send_class(g):
        cg = cls(g)
        for u in range(3):
            rows = pl.ds(pl.multiple_of(cg * 128 + 16 * u, 16), 16)
            tile = kvq[g, rows, 128 * u : 128 * u + 128]
            slp[g, u] = tile
            if g == 3:
                sl[x, z, u] = tile
        slo_copy(g).start()
        if g < 3:
            slz_copy(g).start()
            a2a_copy(g).start()
        else:
            mid[zr] = kvq[g, cls_rows(g), :]

    key = lax.broadcasted_iota(jnp.int32, (1, ROWS), 1)
    inner = 32 * (key % 16) + 4 * ((key // 16) % 8)
    dense_bias = jnp.where(first + inner + key // 128 < length, 0.0, NEG)

    def live(r, width):
        row = lax.broadcasted_iota(jnp.int32, (128, width), 0)
        return first + 32 * (row % 16) + 4 * (row // 16) + r < length

    def dense(g, i):
        cg = cls(g)
        r = (cg + i) % 4
        rows = pl.ds(pl.multiple_of(r * 128, 128), 128)
        o0, o1, l0, l1 = attend3(
            kvq[g, rows, 384:512],
            kvq[g, rows, 512:640],
            lambda u: kvq[g, :, 128 * u : 128 * u + 128],
            dense_bias,
        )
        if i == 0:
            dout[g, :, 0:128] = o0
            dout[g, :, 128:256] = o1
            dlog[g, :, 0:128] = l0
            dlog[g, :, 128:256] = l1
        else:
            ok = live(r, 128)
            attn[cg, rows, 0:128] = jnp.where(ok, o0, 0.0).astype(BF)
            attn[cg, rows, 128:256] = jnp.where(ok, o1, 0.0).astype(BF)

    for g in range(4):
        project(g)
        send_class(g)
        event(g + 1, 4)
        dense(g, 0)
        event(g + 2, 3)
        dense(g, 1)
        event(g + 3, 2)
        dense(g, 2)
        event(g + 4, 1)
        dense(g, 3)
        if g < 3:
            complete(g + 1)

    for g in range(3):
        slz_copy(g).wait_recv()
    for g in range(4):
        slo_copy(g).wait_recv()
    for i in range(3):
        slx_copy(i).start()

    for g in range(3):
        a2a_copy(g).wait_recv()
    group_first = (q // 4) * 4 * ROWS
    mid_bias = jnp.where(group_first + 512 * (key // 128) + inner + zr < length, 0.0, NEG)

    def mid_step(g, carry):
        m = (zr + 3 - g) % 4
        o0, o1, l0, l1 = attend3(
            mid[m, :, 384:512],
            mid[m, :, 512:640],
            lambda u: mid[:, :, 128 * u : 128 * u + 128].reshape(ROWS, 128),
            mid_bias,
        )
        lane = lanes(o0.shape)
        logs = jnp.where(
            lane < 16, pltpu.roll(l0, HEAD, 1), jnp.where(lane < 32, l0, l1)
        )
        logs = jnp.where(lane < 48, split_log(logs, lane), 0.0)
        oret[g, :, 0:128] = o0.astype(BF)
        oret[g, :, 128:256] = jnp.where(lane < HEAD, logs, o1).astype(BF)

        @pl.when(g < 3)
        def _():
            ret_copy(g).start()

        return carry

    lax.fori_loop(0, 4, mid_step, 0)

    for i in range(3):
        slx_copy(i).wait_recv()
    lane64 = lanes((64, 128))
    for u in range(3):
        low = 0 if u != 1 else HEAD
        blk = slice(384, 512) if u < 2 else slice(512, 640)
        qs = mid[:, 16 * u : 16 * u + 16, blk].reshape(64, 128)
        mine = jnp.where(low == 0, lane64, lane64 - HEAD + 128) % 128 < HEAD
        qs = jnp.where(mine, qs, jnp.zeros_like(qs))
        kv = sl[:, :, u].reshape(ROWS, 128)
        bias = jnp.where(32 * key + 4 * u + zr < length, 0.0, NEG)
        o, lg = softmax_block(qs, kv, bias)
        logs = split_log(jnp.broadcast_to(lg, o.shape), lane64)
        packed = jnp.where(mine, logs, o).astype(BF)
        for m in range(4):
            sret[(zr + 3 - m) % 4, u] = packed[16 * m : 16 * m + 16, :]
    for g in range(3):
        srt_copy(g).start()

    complete(4)
    for r in range(4):
        woutp[r, 0:64, :] = woutf[HEAD * (r + 4) : HEAD * (r + 5), :]
        woutp[r, 64:128, :] = woutf[HEAD * r : HEAD * (r + 1), :]
        woutp[r, 128:192, :] = jnp.zeros((64, D), BF)
        woutp[r, 192:256, :] = woutf[HEAD * (r + 8) : HEAD * (r + 9), :]

    def join(logs, outs):
        top = jnp.maximum(jnp.maximum(logs[0], logs[1]), logs[2])
        cs = [jnp.exp(lg - top) for lg in logs]
        num = cs[0] * outs[0] + cs[1] * outs[1] + cs[2] * outs[2]
        return num / (cs[0] + cs[1] + cs[2])

    lane128 = lanes((128, 128))
    lane16 = lanes((16, 128))
    flow = lane128 < HEAD

    def finish(g, mret, sr):
        cg = cls(g)
        rows = cls_rows(g)
        m0 = mret[:, 0:128].astype(F32)
        m1 = mret[:, 128:256].astype(F32)

        def mlog(u):
            hit = jnp.where((lane128 >= 16 * u) & (lane128 < 16 * u + 16), m1, 0.0)
            return jnp.sum(hit, axis=1, keepdims=True)

        ml0 = jnp.where(flow, mlog(1), mlog(0))
        ml1 = jnp.broadcast_to(mlog(2), (128, 128))
        souts = []
        slogs = []
        for u in range(3):
            val = sr(u).astype(F32)
            mine = lane16 >= HEAD if u == 1 else lane16 < HEAD
            first16 = lane16 % HEAD < 16
            lg = jnp.sum(jnp.where(mine & first16, val, 0.0), axis=1, keepdims=True)
            souts.append(jnp.where(mine, 0.0, val))
            slogs.append(jnp.where(mine, -1e30, lg))
        rest = jnp.zeros((80, 128), F32)
        z16 = jnp.zeros((16, 128), F32)
        n16 = jnp.full((16, 128), -1e30, F32)
        nrest = jnp.full((80, 128), -1e30, F32)
        s0 = jnp.concatenate([souts[0], souts[1], z16, rest], axis=0)
        sl0 = jnp.concatenate([slogs[0], slogs[1], n16, nrest], axis=0)
        s1 = jnp.concatenate([z16, z16, souts[2], rest], axis=0)
        sl1 = jnp.concatenate([n16, n16, slogs[2], nrest], axis=0)
        ok = live(cg, 128)
        a0 = join((dlog[g, :, 0:128], ml0, sl0), (dout[g, :, 0:128], m0, s0))
        a1 = join((dlog[g, :, 128:256], ml1, sl1), (dout[g, :, 128:256], m1, s1))
        a1 = jnp.where(flow, 0.0, a1)
        attn[cg, rows, 0:128] = jnp.where(ok, a0, 0.0).astype(BF)
        attn[cg, rows, 128:256] = jnp.where(ok, a1, 0.0).astype(BF)
        res = jnp.dot(attn[0, rows, :], woutp[0], preferred_element_type=F32)
        for r in range(1, 4):
            res = res + jnp.dot(attn[r, rows, :], woutp[r], preferred_element_type=F32)
        for v in range(8):
            for i in range(6):
                outf[i, pl.ds(4 * v + cg, 16, stride=33), :] = res[
                    16 * v : 16 * v + 16, 128 * i : 128 * i + 128
                ]

    finish(3, oret[3], lambda u: sret[3, u])

    for ch in range(5):
        for k in range(4):
            ring_copy(ch, True, k).wait_send()
        for k in range(3):
            ring_copy(ch, False, k).wait_send()
        for i in range(8):
            sib_copy(ch, i).wait_send()
    halo_copy(True).wait_send()
    halo_copy(False).wait_send()
    for g in range(3):
        a2a_copy(g).wait_send()
        slz_copy(g).wait_send()
        slx_copy(g).wait_send()
    for g in range(4):
        slo_copy(g).wait_send()

    for g in range(3):
        ret_copy(g).wait_recv()
        srt_copy(g).wait_recv()
        finish(g, ret[g], lambda u, g=g: srt[g, u])
    for j in range(16):
        for i in range(6):
            out_ref[0, 32 * j : 32 * j + 32, 128 * i : 128 * i + 128] = outf[
                i, 33 * j : 33 * j + 32, :
            ].astype(BF)
    for g in range(3):
        ret_copy(g).wait_send()
        srt_copy(g).wait_send()


def on_device(tokens, slide_lengths, conv_weight, norm_gain, w_query, w_keyvalue, w_out):
    vmem = pl.BlockSpec(memory_space=pltpu.VMEM)
    hbm = pl.BlockSpec(memory_space=pl.ANY)
    dma = pltpu.SemaphoreType.DMA
    return pl.pallas_call(
        kernel,
        out_shape=jax.ShapeDtypeStruct((1, ROWS, D), BF),
        in_specs=[hbm, pl.BlockSpec(memory_space=pltpu.SMEM)] + [hbm] * 5,
        out_specs=vmem,
        scratch_shapes=[
            pltpu.VMEM((1, ROWS, D), BF),
            pltpu.VMEM((TAPS, D), F32),
            pltpu.VMEM((D,), F32),
            pltpu.VMEM((SH, D), BF),
            pltpu.VMEM((SH, 2 * D), BF),
            pltpu.VMEM((SH, D), BF),
            dma((6,)),
            pltpu.VMEM((4, D, CW), BF),
            pltpu.VMEM((D, D), BF),
            pltpu.VMEM((4, 256, D), BF),
            pltpu.VMEM((6, 33 * 18, 128), F32),
            pltpu.VMEM((PAD, D), BF),
            pltpu.VMEM((PAD, D), BF),
            pltpu.VMEM((ROWS, D), BF),
            pltpu.VMEM((4, ROWS, CW), BF),
            pltpu.VMEM((4, 128, CW), BF),
            pltpu.VMEM((4, 3, 16, 128), BF),
            pltpu.VMEM((NX, NZ, 3, 16, 128), BF),
            pltpu.VMEM((4, 128, 256), BF),
            pltpu.VMEM((3, 128, 256), BF),
            pltpu.VMEM((4, 3, 16, 128), BF),
            pltpu.VMEM((3, 3, 16, 128), BF),
            pltpu.VMEM((4, ROWS, 256), BF),
            pltpu.VMEM((4, 128, 256), F32),
            pltpu.VMEM((4, 128, 256), F32),
            pltpu.VMEM((6, 33 * 16, 128), F32),
            dma((5, 7)),
            dma((5, 7)),
            dma((5, 8)),
            dma((5, 8)),
            dma((2,)),
            dma((2,)),
            dma((3,)),
            dma((3,)),
            dma((3,)),
            dma((3,)),
            dma((4,)),
            dma((4,)),
            dma((3,)),
            dma((3,)),
            dma((3,)),
            dma((3,)),
            dma((3,)),
            dma((3,)),
        ],
        compiler_params=pltpu.CompilerParams(
            collective_id=0, has_side_effects=True, vmem_limit_bytes=60 * 1024 * 1024
        ),
        name="layer",
    )(
        tokens,
        slide_lengths,
        conv_weight,
        norm_gain,
        w_query,
        w_keyvalue,
        w_out,
    )


def solution(mesh):
    return jax.shard_map(
        on_device,
        mesh=mesh,
        in_specs=(
            P("batch", "seq", None),
            P("batch"),
            P(),
            P(),
            P("batch", None),
            P("batch", None),
            P("batch", None),
        ),
        out_specs=P("batch", "seq", None),
        check_vma=False,
    )
```

```python
import jax
import jax.numpy as jnp
from jax import lax
from jax.experimental import pallas as pl
from jax.experimental.pallas import tpu as pltpu
from jax.sharding import PartitionSpec as P

HEADS = 12
HEAD = 64
D = 768
ROWS = 512
TAPS = 5
DIL = 3
NY = 8
NX = 4
NZ = 8
SH = 48
CW = 640
PAD = 16
NEG = -1e9
F32 = jnp.float32
BF = jnp.bfloat16
MESH = pl.DeviceIdType.MESH


def lanes(shape):
    return lax.broadcasted_iota(jnp.int32, shape, len(shape) - 1)


def dot_nt(a, b):
    return lax.dot_general(a, b, (((1,), (1,)), ((), ())), preferred_element_type=F32)


def softmax_block(q, kv, bias):
    s = dot_nt(q, kv) + bias
    m = jnp.max(s, axis=1, keepdims=True)
    e = jnp.exp(s - m)
    total = jnp.sum(e, axis=1, keepdims=True)
    o = jnp.dot(e.astype(BF), kv, preferred_element_type=F32)
    return o / total, m + jnp.log(total)


def attend3(qa, qb, kv, bias):
    low = lanes(qa.shape) < HEAD
    zero = jnp.zeros_like(qa)
    qs = (jnp.where(low, qa, zero), jnp.where(low, zero, qa), qb)
    ss = [dot_nt(q, kv(u)) + bias for u, q in enumerate(qs)]
    ms = [jnp.max(s, axis=1, keepdims=True) for s in ss]
    es = [jnp.exp(s - m) for s, m in zip(ss, ms)]
    ts = [jnp.sum(e, axis=1, keepdims=True) for e in es]
    os = [
        jnp.dot(e.astype(BF), kv(u), preferred_element_type=F32) / ts[u]
        for u, e in enumerate(es)
    ]
    ls = [m + jnp.log(t) for m, t in zip(ms, ts)]
    flow = lanes(os[0].shape) < HEAD
    return (
        jnp.where(flow, os[1], os[0]),
        jnp.where(flow, 0.0, os[2]),
        jnp.where(flow, ls[1], ls[0]),
        jnp.broadcast_to(ls[2], os[2].shape),
    )


def split_log(value, lane):
    hi = value.astype(BF).astype(F32)
    rest = value - hi
    mid = rest.astype(BF).astype(F32)
    lo = rest - mid
    place = lane % 16
    return jnp.where(
        place == 0, hi, jnp.where(place == 1, mid, jnp.where(place == 2, lo, 0.0))
    )


def kernel(
    tok_hbm,
    len_ref,
    cw_hbm,
    gain_hbm,
    wq_hbm,
    wkv_hbm,
    wo_hbm,
    out_ref,
    tok_ref,
    cw_ref,
    gain_ref,
    wq_ref,
    wkv_ref,
    wo_ref,
    in_s,
    wfull,
    woutf,
    woutp,
    xp,
    hl,
    hr,
    xn,
    kvq,
    mid,
    slp,
    sl,
    oret,
    ret,
    sret,
    srt,
    attn,
    dout,
    dlog,
    outf,
    pacc,
    ring_s,
    ring_r,
    sib_s,
    sib_r,
    halo_s,
    halo_r,
    a2a_s,
    a2a_r,
    slz_s,
    slz_r,
    slo_s,
    slo_r,
    slx_s,
    slx_r,
    ret_s,
    ret_r,
    srt_s,
    srt_r,
):
    b = lax.axis_index("batch")
    q = lax.axis_index("seq")
    y = b // 2
    c = b % 2
    x = q // NZ
    z = q % NZ
    zr = z % 4
    zg = z // 4
    length = len_ref[0]
    first = q * ROWS

    barrier = pltpu.get_barrier_semaphore()
    friends = [
        (2 * ((y + 1) % NY) + c, q),
        (2 * ((y + NY - 1) % NY) + c, q),
        (2 * y + 1 - c, q),
        (b, (q + 1) % 32),
        (b, (q + 31) % 32),
    ]
    friends += [(b, x * NZ + (z + i) % NZ) for i in range(1, NZ)]
    friends += [(b, ((x + i) % NX) * NZ + z) for i in range(1, NX)]
    for friend in friends:
        pl.semaphore_signal(barrier, inc=1, device_id=friend, device_id_type=MESH)

    loads = [
        pltpu.make_async_copy(src, dst, in_s.at[i])
        for i, (src, dst) in enumerate(
            (
                (wkv_hbm, wkv_ref),
                (wq_hbm, wq_ref),
                (wo_hbm, wo_ref),
                (tok_hbm, tok_ref),
                (cw_hbm, cw_ref),
                (gain_hbm, gain_ref),
            )
        )
    ]
    for load in loads:
        load.start()
    for load in loads[:3]:
        load.wait()

    own_rows = pl.ds(pl.multiple_of(b * SH, 16), SH)
    wlane = lanes((SH, 128)) < HEAD

    def half(ref, col, upper):
        block = ref[:, (col // 128) * 128 : (col // 128) * 128 + 128].astype(F32)
        if (col % 128 == HEAD) != upper:
            block = pltpu.roll(block, HEAD, 1)
        return block

    def place(r, i, low, high):
        wfull[r, own_rows, 128 * i : 128 * i + 128] = jnp.where(wlane, low, high).astype(BF)

    for r in range(4):
        h0, h1, h2 = HEAD * r, HEAD * (r + 4), HEAD * (r + 8)
        place(r, 0, half(wkv_ref, h0, False), half(wkv_ref, D + h0, True))
        place(r, 1, half(wkv_ref, D + h1, False), half(wkv_ref, h1, True))
        place(r, 2, half(wkv_ref, h2, False), half(wkv_ref, D + h2, True))
        place(r, 3, half(wq_ref, h0, False), half(wq_ref, h1, True))
        place(r, 4, half(wq_ref, h2, False), jnp.zeros((SH, 128), F32))
    woutf[own_rows, :] = wo_ref[...]

    def cls(g):
        return (zr + g + 1) % 4

    def mask_tokens():
        for j in range(16):
            pos = first + 32 * j + lax.broadcasted_iota(jnp.int32, (32, 128), 0)
            ok = pos < length
            for i in range(6):
                tile = tok_ref[0, 32 * j : 32 * j + 32, 128 * i : 128 * i + 128]
                xp[i, 33 * j + 33 : 33 * j + 65, :] = jnp.where(ok, tile.astype(F32), 0.0)

    way = 1 - 2 * c

    def shard(ch, yo, co):
        rows = pl.ds(pl.multiple_of((2 * yo + co) * SH, 16), SH)
        if ch < 4:
            return wfull.at[cls(ch), rows, :]
        return woutf.at[rows, :]

    def ring_copy(ch, long, k):
        d = way if long else -way
        part = shard(ch, (y + NY - k * d) % NY, c)
        i = k if long else 4 + k
        return pltpu.make_async_remote_copy(
            src_ref=part,
            dst_ref=part,
            send_sem=ring_s.at[ch, i],
            recv_sem=ring_r.at[ch, i],
            device_id=(2 * ((y + NY + d) % NY) + c, q),
            device_id_type=MESH,
        )

    def sib_copy(ch, i):
        step = -i * way if i <= 4 else (i - 4) * way
        part = shard(ch, (y + NY + step) % NY, c)
        return pltpu.make_async_remote_copy(
            src_ref=part,
            dst_ref=part,
            send_sem=sib_s.at[ch, i],
            recv_sem=sib_r.at[ch, i],
            device_id=(2 * y + 1 - c, q),
            device_id_type=MESH,
        )

    def event(ch, k):
        if ch > 4:
            return
        if k == 0:
            ring_copy(ch, True, 0).start()
            ring_copy(ch, False, 0).start()
            sib_copy(ch, 0).start()
            return
        ring_copy(ch, True, k - 1).wait_recv()
        if k <= 3:
            ring_copy(ch, True, k).start()
        sib_copy(ch, k).start()
        if k <= 3:
            ring_copy(ch, False, k - 1).wait_recv()
            if k <= 2:
                ring_copy(ch, False, k).start()
            sib_copy(ch, 4 + k).start()

    def complete(ch):
        for i in range(8):
            sib_copy(ch, i).wait_recv()

    def halo_copy(right):
        if right:
            src, dst, i, to = tok_ref.at[0, pl.ds(ROWS - PAD, PAD), :], hl, 0, (q + 1) % 32
        else:
            src, dst, i, to = tok_ref.at[0, pl.ds(0, PAD), :], hr, 1, (q + 31) % 32
        return pltpu.make_async_remote_copy(
            src_ref=src,
            dst_ref=dst,
            send_sem=halo_s.at[i],
            recv_sem=halo_r.at[i],
            device_id=(b, to),
            device_id_type=MESH,
        )

    for load in loads[3:]:
        load.wait()
    mask_tokens()
    pl.semaphore_wait(barrier, len(friends))
    event(0, 0)
    halo_copy(True).start()
    halo_copy(False).start()
    event(1, 0)

    def conv(s):
        parts = []
        for i in range(6):
            cols = slice(128 * i, 128 * i + 128)
            acc = xp[i, pl.ds(33 + s, 16, stride=33), :]
            for t in range(TAPS):
                at = 32 + s + (t - TAPS // 2) * DIL
                tap = xp[i, pl.ds(33 * (at // 32) + at % 32, 16, stride=33), :]
                acc = acc + cw_ref[t : t + 1, cols] * tap
            parts.append(acc)
        total = parts[0]
        for part in parts[1:]:
            total = total + part
        mean = jnp.sum(total, axis=1, keepdims=True) * (1.0 / D)
        parts = [part - mean for part in parts]
        square = parts[0] * parts[0]
        for part in parts[1:]:
            square = square + part * part
        scale = lax.rsqrt(jnp.sum(square, axis=1, keepdims=True) * (1.0 / D) + 1e-5)
        row = pl.multiple_of(((s % 4) * 8 + s // 4) * 16, 16)
        for i in range(6):
            cols = slice(128 * i, 128 * i + 128)
            xn[pl.ds(row, 16), cols] = (parts[i] * scale * gain_ref[cols].reshape(1, 128)).astype(BF)

    def conv_range(lo, hi):
        def step(s, carry):
            conv(lo + 2 * s)
            conv(lo + 2 * s + 1)
            return carry

        lax.fori_loop(0, (hi - lo) // 2, step, 0)

    conv_range(6, 16)
    event(0, 1)
    conv_range(16, 26)
    event(1, 1)
    event(2, 0)
    event(0, 2)
    halo_copy(True).wait_recv()
    halo_copy(False).wait_recv()
    for i in range(6):
        cols = slice(128 * i, 128 * i + 128)
        off = lax.broadcasted_iota(jnp.int32, (PAD, 128), 0)
        left = first - PAD + off
        right = first + ROWS + off
        left_ok = jnp.where(left >= 0, left, length) < length
        xp[i, 16:32, :] = jnp.where(left_ok, hl[:, cols].astype(F32), 0.0)
        xp[i, 561:577, :] = jnp.where(
            right < length, hr[:, cols].astype(F32), 0.0
        )
    conv_range(0, 6)
    event(1, 2)
    event(0, 3)
    event(2, 1)
    event(3, 0)
    conv_range(26, 32)
    event(1, 3)
    event(0, 4)
    event(2, 2)
    event(3, 1)
    event(4, 0)
    complete(0)

    def project(g):
        cg = cls(g)

        def step(i, carry):
            rows = pl.ds(pl.multiple_of(i * 256, 256), 256)
            res = jnp.dot(xn[rows, :], wfull[cg], preferred_element_type=F32)
            res = jnp.where(lanes(res.shape) < 384, res, res * (1.0 / 8.0))
            kvq[g, rows, :] = res.astype(BF)
            return carry

        lax.fori_loop(0, 2, step, 0)

    def cls_rows(g):
        return pl.ds(pl.multiple_of(cls(g) * 128, 128), 128)

    def a2a_copy(g):
        return pltpu.make_async_remote_copy(
            src_ref=kvq.at[g, cls_rows(g), :],
            dst_ref=mid.at[zr],
            send_sem=a2a_s.at[g],
            recv_sem=a2a_r.at[g],
            device_id=(b, x * NZ + zg * 4 + cls(g)),
            device_id_type=MESH,
        )

    def slz_copy(g):
        return pltpu.make_async_remote_copy(
            src_ref=slp.at[g],
            dst_ref=sl.at[x, zr, zg],
            send_sem=slz_s.at[g],
            recv_sem=slz_r.at[g],
            device_id=(b, x * NZ + zg * 4 + cls(g)),
            device_id_type=MESH,
        )

    def slo_copy(g):
        return pltpu.make_async_remote_copy(
            src_ref=slp.at[g],
            dst_ref=sl.at[x, zr, zg],
            send_sem=slo_s.at[g],
            recv_sem=slo_r.at[g],
            device_id=(b, x * NZ + (1 - zg) * 4 + cls(g)),
            device_id_type=MESH,
        )

    def slx_copy(g, i):
        part = sl.at[x, (zr + 3 - g) % 4]
        return pltpu.make_async_remote_copy(
            src_ref=part,
            dst_ref=part,
            send_sem=slx_s.at[g, i],
            recv_sem=slx_r.at[g, i],
            device_id=(b, ((x + i + 1) % NX) * NZ + z),
            device_id_type=MESH,
        )

    def back(g):
        return (b, x * NZ + zg * 4 + (zr + 3 - g) % 4)

    def ret_copy(g):
        return pltpu.make_async_remote_copy(
            src_ref=oret.at[g],
            dst_ref=ret.at[g],
            send_sem=ret_s.at[g],
            recv_sem=ret_r.at[g],
            device_id=back(g),
            device_id_type=MESH,
        )

    def srt_copy(g):
        return pltpu.make_async_remote_copy(
            src_ref=sret.at[g],
            dst_ref=srt.at[g],
            send_sem=srt_s.at[g],
            recv_sem=srt_r.at[g],
            device_id=back(g),
            device_id_type=MESH,
        )

    def send_class(g):
        cg = cls(g)
        for u in range(3):
            rows = pl.ds(pl.multiple_of(cg * 128 + 16 * u, 16), 16)
            tile = kvq[g, rows, 128 * u : 128 * u + 128]
            slp[g, u] = tile
            if g == 3:
                sl[x, zr, zg, u] = tile
        slo_copy(g).start()
        if g < 3:
            slz_copy(g).start()
            a2a_copy(g).start()
        else:
            mid[zr] = kvq[g, cls_rows(g), :]

    key = lax.broadcasted_iota(jnp.int32, (1, ROWS), 1)
    inner = 32 * (key % 16) + 4 * ((key // 16) % 8)
    dense_bias = jnp.where(first + inner + key // 128 < length, 0.0, NEG)

    def live(r, width):
        row = lax.broadcasted_iota(jnp.int32, (128, width), 0)
        return first + 32 * (row % 16) + 4 * (row // 16) + r < length

    def dense(g, i):
        cg = cls(g)
        two = [(cg + 2 * i) % 4, (cg + 2 * i + 1) % 4]
        rows = [pl.ds(pl.multiple_of(r * 128, 128), 128) for r in two]
        o0, o1, l0, l1 = attend3(
            jnp.concatenate([kvq[g, rows[0], 384:512], kvq[g, rows[1], 384:512]], axis=0),
            jnp.concatenate([kvq[g, rows[0], 512:640], kvq[g, rows[1], 512:640]], axis=0),
            lambda u: kvq[g, :, 128 * u : 128 * u + 128],
            dense_bias,
        )
        for n in range(2):
            part = slice(128 * n, 128 * n + 128)
            if i == 0 and n == 0:
                dout[g, :, 0:128] = o0[part]
                dout[g, :, 128:256] = o1[part]
                dlog[g, :, 0:128] = l0[part]
                dlog[g, :, 128:256] = l1[part]
            else:
                ok = live(two[n], 128)
                attn[cg, rows[n], 0:128] = jnp.where(ok, o0[part], 0.0).astype(BF)
                attn[cg, rows[n], 128:256] = jnp.where(ok, o1[part], 0.0).astype(BF)

    group_first = (q // 4) * 4 * ROWS
    mid_bias = jnp.where(group_first + 512 * (key // 128) + inner + zr < length, 0.0, NEG)

    def middle(pair):
        gs = (2 * pair, 2 * pair + 1)
        src = [(zr + 3 - g) % 4 for g in gs]
        o0, o1, l0, l1 = attend3(
            jnp.concatenate([mid[m, :, 384:512] for m in src], axis=0),
            jnp.concatenate([mid[m, :, 512:640] for m in src], axis=0),
            lambda u: mid[:, :, 128 * u : 128 * u + 128].reshape(ROWS, 128),
            mid_bias,
        )
        lane = lanes(o0.shape)
        logs = jnp.where(
            lane < 16, pltpu.roll(l0, HEAD, 1), jnp.where(lane < 32, l0, l1)
        )
        logs = jnp.where(lane < 48, split_log(logs, lane), 0.0)
        o1 = jnp.where(lane < HEAD, logs, o1).astype(BF)
        o0 = o0.astype(BF)
        for n, g in enumerate(gs):
            part = slice(128 * n, 128 * n + 128)
            oret[g, :, 0:128] = o0[part]
            oret[g, :, 128:256] = o1[part]
            if g < 3:
                ret_copy(g).start()

    def slide_out(g):
        if g < 3:
            slz_copy(g).wait_recv()
        slo_copy(g).wait_recv()
        for i in range(3):
            slx_copy(g, i).start()

    for g in range(4):
        project(g)
        send_class(g)
        event(g + 1, 4)
        dense(g, 0)
        event(g + 2, 3)
        event(g + 3, 2)
        if g > 0:
            slide_out(g - 1)
        dense(g, 1)
        event(g + 4, 1)
        if g < 3:
            complete(g + 1)
    slide_out(3)
    for g in range(3):
        a2a_copy(g).wait_recv()
    middle(0)
    middle(1)

    complete(4)
    for r in range(4):
        woutp[r, 0:64, :] = woutf[HEAD * (r + 4) : HEAD * (r + 5), :]
        woutp[r, 64:128, :] = woutf[HEAD * r : HEAD * (r + 1), :]
        woutp[r, 128:192, :] = jnp.zeros((64, D), BF)
        woutp[r, 192:256, :] = woutf[HEAD * (r + 8) : HEAD * (r + 9), :]

    def partial(g):
        res = None
        for k in range(1, 4):
            r = cls(g + k)
            term = jnp.dot(attn[r, cls_rows(g), :], woutp[r], preferred_element_type=F32)
            res = term if res is None else res + term
        pacc[g] = res

    for g in range(4):
        partial(g)

    for g in range(4):
        for i in range(3):
            slx_copy(g, i).wait_recv()
    lane64 = lanes((64, 128))
    for u in range(3):
        low = 0 if u != 1 else HEAD
        blk = slice(384, 512) if u < 2 else slice(512, 640)
        qs = mid[:, 16 * u : 16 * u + 16, blk].reshape(64, 128)
        mine = jnp.where(low == 0, lane64, lane64 - HEAD + 128) % 128 < HEAD
        qs = jnp.where(mine, qs, jnp.zeros_like(qs))
        kv = sl[:, :, :, u].reshape(ROWS, 128)
        device = NZ * (key // 128) + 4 * ((key // 16) % 2) + (key // 32) % 4
        bias = jnp.where(512 * device + 32 * (key % 16) + 4 * u + zr < length, 0.0, NEG)
        o, lg = softmax_block(qs, kv, bias)
        logs = split_log(jnp.broadcast_to(lg, o.shape), lane64)
        packed = jnp.where(mine, logs, o).astype(BF)
        for m in range(4):
            sret[(zr + 3 - m) % 4, u] = packed[16 * m : 16 * m + 16, :]
    for g in range(3):
        srt_copy(g).start()

    def join(logs, outs):
        top = jnp.maximum(jnp.maximum(logs[0], logs[1]), logs[2])
        cs = [jnp.exp(lg - top) for lg in logs]
        num = cs[0] * outs[0] + cs[1] * outs[1] + cs[2] * outs[2]
        return num / (cs[0] + cs[1] + cs[2])

    lane128 = lanes((128, 128))
    lane16 = lanes((16, 128))
    flow = lane128 < HEAD

    def finish(g, mret, sr):
        cg = cls(g)
        m0 = mret[:, 0:128].astype(F32)
        m1 = mret[:, 128:256].astype(F32)

        def mlog(u):
            hit = jnp.where((lane128 >= 16 * u) & (lane128 < 16 * u + 16), m1, 0.0)
            return jnp.sum(hit, axis=1, keepdims=True)

        ml0 = jnp.where(flow, mlog(1), mlog(0))
        ml1 = jnp.broadcast_to(mlog(2), (128, 128))
        souts = []
        slogs = []
        for u in range(3):
            val = sr(u).astype(F32)
            mine = lane16 >= HEAD if u == 1 else lane16 < HEAD
            first16 = lane16 % HEAD < 16
            lg = jnp.sum(jnp.where(mine & first16, val, 0.0), axis=1, keepdims=True)
            souts.append(jnp.where(mine, 0.0, val))
            slogs.append(jnp.where(mine, -1e30, lg))
        rest = jnp.zeros((80, 128), F32)
        z16 = jnp.zeros((16, 128), F32)
        n16 = jnp.full((16, 128), -1e30, F32)
        nrest = jnp.full((80, 128), -1e30, F32)
        s0 = jnp.concatenate([souts[0], souts[1], z16, rest], axis=0)
        sl0 = jnp.concatenate([slogs[0], slogs[1], n16, nrest], axis=0)
        s1 = jnp.concatenate([z16, z16, souts[2], rest], axis=0)
        sl1 = jnp.concatenate([n16, n16, slogs[2], nrest], axis=0)
        ok = live(cg, 128)
        a0 = join((dlog[g, :, 0:128], ml0, sl0), (dout[g, :, 0:128], m0, s0))
        a1 = join((dlog[g, :, 128:256], ml1, sl1), (dout[g, :, 128:256], m1, s1))
        a1 = jnp.where(flow, 0.0, a1)
        row = jnp.concatenate(
            [jnp.where(ok, a0, 0.0).astype(BF), jnp.where(ok, a1, 0.0).astype(BF)], axis=1
        )
        res = pacc[g] + jnp.dot(row, woutp[cg], preferred_element_type=F32)
        for v in range(8):
            for i in range(6):
                outf[i, pl.ds(4 * v + cg, 16, stride=33), :] = res[
                    16 * v : 16 * v + 16, 128 * i : 128 * i + 128
                ]

    finish(3, oret[3], lambda u: sret[3, u])

    for ch in range(5):
        for k in range(4):
            ring_copy(ch, True, k).wait_send()
        for k in range(3):
            ring_copy(ch, False, k).wait_send()
        for i in range(8):
            sib_copy(ch, i).wait_send()
    halo_copy(True).wait_send()
    halo_copy(False).wait_send()
    for g in range(3):
        a2a_copy(g).wait_send()
        slz_copy(g).wait_send()
    for g in range(4):
        slo_copy(g).wait_send()
        for i in range(3):
            slx_copy(g, i).wait_send()

    for g in range(3):
        ret_copy(g).wait_recv()
        srt_copy(g).wait_recv()
        finish(g, ret[g], lambda u, g=g: srt[g, u])
    for j in range(16):
        for i in range(6):
            out_ref[0, 32 * j : 32 * j + 32, 128 * i : 128 * i + 128] = outf[
                i, 33 * j : 33 * j + 32, :
            ].astype(BF)
    for g in range(3):
        ret_copy(g).wait_send()
        srt_copy(g).wait_send()


def on_device(tokens, slide_lengths, conv_weight, norm_gain, w_query, w_keyvalue, w_out):
    vmem = pl.BlockSpec(memory_space=pltpu.VMEM)
    hbm = pl.BlockSpec(memory_space=pl.ANY)
    dma = pltpu.SemaphoreType.DMA
    return pl.pallas_call(
        kernel,
        out_shape=jax.ShapeDtypeStruct((1, ROWS, D), BF),
        in_specs=[hbm, pl.BlockSpec(memory_space=pltpu.SMEM)] + [hbm] * 5,
        out_specs=vmem,
        scratch_shapes=[
            pltpu.VMEM((1, ROWS, D), BF),
            pltpu.VMEM((TAPS, D), F32),
            pltpu.VMEM((D,), F32),
            pltpu.VMEM((SH, D), BF),
            pltpu.VMEM((SH, 2 * D), BF),
            pltpu.VMEM((SH, D), BF),
            dma((6,)),
            pltpu.VMEM((4, D, CW), BF),
            pltpu.VMEM((D, D), BF),
            pltpu.VMEM((4, 256, D), BF),
            pltpu.VMEM((6, 33 * 18, 128), F32),
            pltpu.VMEM((PAD, D), BF),
            pltpu.VMEM((PAD, D), BF),
            pltpu.VMEM((ROWS, D), BF),
            pltpu.VMEM((4, ROWS, CW), BF),
            pltpu.VMEM((4, 128, CW), BF),
            pltpu.VMEM((4, 3, 16, 128), BF),
            pltpu.VMEM((NX, 4, 2, 3, 16, 128), BF),
            pltpu.VMEM((4, 128, 256), BF),
            pltpu.VMEM((3, 128, 256), BF),
            pltpu.VMEM((4, 3, 16, 128), BF),
            pltpu.VMEM((3, 3, 16, 128), BF),
            pltpu.VMEM((4, ROWS, 256), BF),
            pltpu.VMEM((4, 128, 256), F32),
            pltpu.VMEM((4, 128, 256), F32),
            pltpu.VMEM((6, 33 * 16, 128), F32),
            pltpu.VMEM((4, 128, D), F32),
            dma((5, 7)),
            dma((5, 7)),
            dma((5, 8)),
            dma((5, 8)),
            dma((2,)),
            dma((2,)),
            dma((3,)),
            dma((3,)),
            dma((3,)),
            dma((3,)),
            dma((4,)),
            dma((4,)),
            dma((4, 3)),
            dma((4, 3)),
            dma((3,)),
            dma((3,)),
            dma((3,)),
            dma((3,)),
        ],
        compiler_params=pltpu.CompilerParams(
            collective_id=0, has_side_effects=True, vmem_limit_bytes=60 * 1024 * 1024
        ),
        name="layer",
    )(
        tokens,
        slide_lengths,
        conv_weight,
        norm_gain,
        w_query,
        w_keyvalue,
        w_out,
    )


def solution(mesh):
    return jax.shard_map(
        on_device,
        mesh=mesh,
        in_specs=(
            P("batch", "seq", None),
            P("batch"),
            P(),
            P(),
            P("batch", None),
            P("batch", None),
            P("batch", None),
        ),
        out_specs=P("batch", "seq", None),
        check_vma=False,
    )
```
